32 devices in a mesh: dp: 4 (over z), row: 2 (over core), col: 4 (over y, x).
Axes of the slice: x: 2, y: 2, z: 4, core: 2. Of those that a mesh axis runs over, the one named last changes fastest.
Arguments:
- states: bfloat16 [16384, 768], P(('dp', 'col'), 'row'), may hold values from -6 to 6
- teacher: bfloat16 [16384, 768], P(('dp', 'col'), 'row'), may hold values from -6 to 6
- valid_mask: int32 [16384], P('dp'), may hold values from 0 to 1, as said below
- seg_ids: int32 [8, 2048], P(('dp', 'row')), may hold values from 0 to 3, never falling along the last dimension, each value on 1 to 1024 neighbouring positions
- piece_start: int32 [8, 2048], P(('dp', 'row')), may hold values from -256 to 1792, as said below
- norm1_gain: float32 [768], P('row'), may hold values from 0.5 to 1.5
- norm1_bias: float32 [768], P('row'), may hold values from -0.75 to 0.75
- w_qkv: bfloat16 [768, 3, 768], P('row', None, 'col'), may hold values from -0.21875 to 0.21875
- b_qv: float32 [2, 768], P(None, 'col'), may hold values from -0.75 to 0.75
- w_out: bfloat16 [768, 768], P('col', 'row'), may hold values from -1.75 to 1.75
- b_out: float32 [768], P('row'), may hold values from -4 to 4
- norm2_gain: float32 [768], P('row'), may hold values from 0.5 to 1.5
- norm2_bias: float32 [768], P('row'), may hold values from -0.75 to 0.75
- w_up: bfloat16 [768, 3072], P('row', 'col'), may hold values from -0.21875 to 0.21875
- b_up: float32 [3072], P('col'), may hold values from -4 to 4
- w_down: bfloat16 [3072, 768], P('col', 'row'), may hold values from -0.15625 to 0.15625
- b_down: float32 [768], P('row'), may hold values from -4 to 4
Outputs:
- out: bfloat16 [16384, 768], P(('dp', 'col'), 'row')
- loss: float32 [], replicated
- grad_x: float32 [16384, 768], P(('dp', 'col'), 'row')
- grad_norm1_gain: float32 [768], P('row')
- grad_norm1_bias: float32 [768], P('row')
- grad_w_qkv: float32 [768, 3, 768], P('row', None, 'col')
- grad_b_qv: float32 [2, 768], P(None, 'col')
- grad_w_out: float32 [768, 768], P('col', 'row')
- grad_b_out: float32 [768], P('row')
- grad_norm2_gain: float32 [768], P('row')
- grad_norm2_bias: float32 [768], P('row')
- grad_w_up: float32 [768, 3072], P('row', 'col')
- grad_b_up: float32 [3072], P('col')
- grad_w_down: float32 [3072, 768], P('col', 'row')
- grad_b_down: float32 [768], P('row')
The draws below stay inside these ranges and needn't reach their ends.
Inputs may be any that keep to these rules, and one draw needn't show every extreme that they name: `valid_mask`: the first token of every sequence is valid. `seg_ids`: documents of a sequence are runs of positions; the number never falls along a sequence. `piece_start`: pieces are aligned runs of 256 positions, and every token of a piece holds the piece's first position; a token in causal text holds minus 256; in every sequence the first 256 positions are causal text and the last 256 form a piece.
All inputs are finite; a program needn't handle non-finite values.
Results may differ from the reference program's by a relative error of at most 0.009.
Values may be sent and summed in bfloat16 or wider, within the bound.
No kernel may reach another device: no remote copies, remote signals or barrier semaphores. Data moves between devices by JAX's collectives and lax.ppermute only.
A program may use at most 128 MiB of HBM per device.

```python
import math
import jax
import jax.numpy as jnp
import numpy as np
from jax import lax

D = 768
HEADS = 12
DH = 64
FF = 3072
LEN = 2048
PIECE = 256
SEGS = 4
NSEQ = 8
TOKENS = 16384


def draw_valid_mask(key, part):
    places = jnp.arange(TOKENS, dtype=jnp.int32)
    seq_index = places // LEN
    threshold = 30 + 65 * seq_index // max(NSEQ - 1, 1)
    rolled = jax.random.randint(key, (TOKENS,), 0, 100)
    first = places % LEN == 0
    return jnp.where((rolled < threshold) | first, 1, 0).astype(jnp.int32)


def draw_piece_start(key, part):
    blocks = LEN // PIECE
    picked = jax.random.randint(key, (NSEQ, blocks), 0, 2)
    block_index = jnp.arange(blocks, dtype=jnp.int32)
    picked = jnp.where(block_index[None, :] == blocks - 1, 1, jnp.where(block_index[None, :] == 0, 0, picked))
    starts = jnp.where(picked > 0, block_index[None, :] * PIECE, -PIECE)
    return jnp.repeat(starts, PIECE, axis=1).astype(jnp.int32)


def block_levels(key, shape, cuts, least, largest):
    level = 1.0
    for axis_at, blocks in cuts:
        draws = jax.random.uniform(jax.random.fold_in(jax.random.fold_in(key, 6), axis_at), (blocks,), jnp.float32, least / len(cuts), largest / len(cuts))
        level = level * jnp.repeat(jnp.exp(draws), shape[axis_at] // blocks).reshape((-1,) + (1,) * (len(shape) - 1 - axis_at))
    return level


def split_up(amount, total, limit, slope):
    loads = [(1 << 20) // math.isqrt(rank ** slope) + 1 for rank in range(2, amount + 1)]
    spare, holding = total - limit - (amount - 1), [1] * (amount - 1)
    while spare > 0:
        movable = [i for i in range(amount - 1) if holding[i] < limit]
        mass, budget = sum([loads[i] for i in movable]), spare
        for i in movable:
            more = min(limit - holding[i], max(1, budget * loads[i] // mass), spare)
            holding[i] = holding[i] + more
            spare = spare - more
    return np.array([limit] + holding)


def uneven_parts(stream_key, amount, total, bound, lean):
    if amount == 2:
        one = jax.random.randint(stream_key, (), max(1, total - bound), min(bound, total - 1) + 1)
        return jnp.stack([one, total - one])
    lengths = jnp.asarray(split_up(amount, total, bound, lean), jnp.int32)
    pairs = (amount - 1) // 2
    donor, taker = lengths[1:1 + 2 * pairs:2], lengths[2:2 + 2 * pairs:2]
    room = jnp.minimum(donor - 1, bound - taker)
    shifted = jax.random.randint(jax.random.fold_in(stream_key, 1), (pairs,), 0, 1 << 20) % (room + 1)
    lengths = lengths.at[1:1 + 2 * pairs:2].set(donor - shifted).at[2:2 + 2 * pairs:2].set(taker + shifted)
    return lengths[jax.random.permutation(jax.random.fold_in(stream_key, 2), amount)]


def gaussian(rng, extent, width, most, split=(), kind=jnp.bfloat16):
    entries = jax.random.normal(rng, extent, jnp.float32) * width
    if len(split) > 0:
        entries = block_levels(rng, extent, split, -0.22, 0.18) * entries
    return jnp.clip(entries, min=-most, max=most).astype(kind)


def setup_inputs(seed: int = 0) -> dict:
    key_of = jax.random.split(jax.random.key(seed), 18)
    states = gaussian(key_of[0], (TOKENS, D), 1.0, 6.0, ((0, 16), (1, 2)))
    teacher = gaussian(key_of[1], (TOKENS, D), 1.0, 6.0, ((0, 16), (1, 2)))
    valid_mask = draw_valid_mask(jax.random.fold_in(key_of[17], 71), 0)
    seg_ids = jax.vmap(lambda own: jnp.searchsorted(jnp.cumsum(uneven_parts(own, SEGS, LEN, LEN // 2, 1)), jnp.arange(LEN), side="right"))(jax.random.split(key_of[3], NSEQ)).reshape((NSEQ, LEN)).astype(jnp.int32)
    piece_start = draw_piece_start(jax.random.fold_in(key_of[17], 71), 0)
    norm1_gain = jnp.clip(1.0 + 0.1 * jax.random.normal(key_of[5], (D,), jnp.float32), 0.5, 1.5)
    norm1_bias = gaussian(key_of[6], (D,), 0.05, 0.75, ((0, 2),), jnp.float32)
    w_qkv = gaussian(key_of[7], (D, 3, D), D ** -0.5, 0.21875, ((0, 2), (2, 4)))
    b_qv = gaussian(key_of[8], (2, D), 0.05, 0.75, ((1, 4),), jnp.float32)
    w_out = gaussian(key_of[9], (D, D), (D // 64) ** -0.5, 1.75, ((0, 4), (1, 2)))
    b_out = gaussian(key_of[10], (D,), 0.3, 4.0, ((0, 2),), jnp.float32)
    norm2_gain = jnp.clip(1.0 + 0.1 * jax.random.normal(key_of[11], (D,), jnp.float32), 0.5, 1.5)
    norm2_bias = gaussian(key_of[12], (D,), 0.05, 0.75, ((0, 2),), jnp.float32)
    w_up = gaussian(key_of[13], (D, FF), D ** -0.5, 0.21875, ((0, 2), (1, 4)))
    b_up = gaussian(key_of[14], (FF,), 0.3, 4.0, ((0, 4),), jnp.float32)
    w_down = gaussian(key_of[15], (FF, D), (FF // 2) ** -0.5, 0.15625, ((0, 4), (1, 2)))
    b_down = gaussian(key_of[16], (D,), 0.3, 4.0, ((0, 2),), jnp.float32)
    return dict(states=states, teacher=teacher, valid_mask=valid_mask, seg_ids=seg_ids, piece_start=piece_start, norm1_gain=norm1_gain, norm1_bias=norm1_bias, w_qkv=w_qkv, b_qv=b_qv, w_out=w_out, b_out=b_out, norm2_gain=norm2_gain, norm2_bias=norm2_bias, w_up=w_up, b_up=b_up, w_down=w_down, b_down=b_down)


@jax.custom_vjp
def low(v):
    return lax.optimization_barrier(v.astype(jnp.bfloat16)).astype(jnp.float32)

@jax.custom_vjp
def low_back(v):
    return v

def low_keep(v):
    return (low(v), None)

def low_pass(kept, grad):
    return (grad,)

def back_keep(v):
    return (v, None)

def back_low(kept, grad):
    return (low(grad),)
low.defvjp(low_keep, low_pass)
low_back.defvjp(back_keep, back_low)
norm_eps = 1e-06
highest = lax.Precision.HIGHEST

def layer_norm(values, gain, shift):
    center = lax.optimization_barrier(jnp.mean(values, axis=-1, keepdims=True))
    spread = lax.optimization_barrier(jnp.mean(values * values, axis=-1, keepdims=True)) - center * center
    return (values - center) * lax.rsqrt(spread + norm_eps) * gain + shift

def attend_one(pieces):
    query, keys, values, seg_row, mask_row, start_row = pieces
    places = jnp.arange(LEN).astype(jnp.int32)
    reach = jnp.maximum(places, start_row.astype(jnp.int32) + PIECE - 1)
    allowed = (seg_row[:, None] == seg_row[None, :]) & ((mask_row[None, :] > 0) | (places[:, None] == places[None, :])) & (places[None, :] <= reach[:, None])
    query_heads = query.reshape(LEN, HEADS, DH)
    key_heads = keys.reshape(LEN, HEADS, DH)
    value_heads = values.reshape(LEN, HEADS, DH)
    scores = jnp.einsum('qhd,khd->hqk', query_heads, key_heads, precision=highest) * DH ** (-0.5)
    scores = low_back(jnp.where(allowed[None], scores, -1e+30))
    probs = low(jax.nn.softmax(scores, axis=-1))
    mixed = jnp.einsum('hqk,khd->qhd', probs, value_heads, precision=highest)
    return mixed.reshape(LEN, D)

def forward(states, norm1_gain, norm1_bias, w_qkv, b_qv, w_out, b_out, norm2_gain, norm2_bias, w_up, b_up, w_down, b_down, teacher, valid_f, seg_ids, piece_start):
    hidden1 = low(layer_norm(states, norm1_gain, norm1_bias))
    projected = jnp.einsum('td,dme->tme', hidden1, w_qkv, precision=highest)
    query = low_back(low(projected[:, 0] + b_qv[0]))
    keys = low_back(low(projected[:, 1]))
    values = low_back(low(projected[:, 2] + b_qv[1]))
    mixed = lax.map(jax.checkpoint(attend_one), (query.reshape(NSEQ, LEN, D), keys.reshape(NSEQ, LEN, D), values.reshape(NSEQ, LEN, D), seg_ids, valid_f.reshape(NSEQ, LEN), piece_start))
    attended = low_back(low(mixed.reshape(TOKENS, D)))
    middle = states + low_back(jnp.dot(attended, w_out, precision=highest) + b_out)
    hidden2 = low(layer_norm(middle, norm2_gain, norm2_bias))
    upper = low_back(jnp.dot(hidden2, w_up, precision=highest) + b_up)
    act = low(jax.nn.gelu(upper, approximate=False))
    result = middle + low_back(jnp.dot(act, w_down, precision=highest) + b_down)
    diff = (result - teacher) * valid_f[:, None]
    count = jnp.sum(valid_f)
    loss = jnp.sum(diff * diff) / (count * D)
    return (result, loss)

def reference(states, teacher, valid_mask, seg_ids, piece_start, norm1_gain, norm1_bias, w_qkv, b_qv, w_out, b_out, norm2_gain, norm2_bias, w_up, b_up, w_down, b_down):
    teacher_f = teacher.astype(jnp.float32)
    valid_f = valid_mask.astype(jnp.float32)

    def objective(states_f, gain1, shift1, wqkv, bqv, wout, bout, gain2, shift2, wup, bup, wdown, bdown):
        return forward(states_f, gain1, shift1, wqkv, bqv, wout, bout, gain2, shift2, wup, bup, wdown, bdown, teacher_f, valid_f, seg_ids, piece_start)
    (result, loss), pull = jax.vjp(objective, states.astype(jnp.float32), norm1_gain.astype(jnp.float32), norm1_bias.astype(jnp.float32), w_qkv.astype(jnp.float32), b_qv.astype(jnp.float32), w_out.astype(jnp.float32), b_out.astype(jnp.float32), norm2_gain.astype(jnp.float32), norm2_bias.astype(jnp.float32), w_up.astype(jnp.float32), b_up.astype(jnp.float32), w_down.astype(jnp.float32), b_down.astype(jnp.float32))
    grads = pull((jnp.zeros_like(result), jnp.ones_like(loss) * (TOKENS * D / 2)))
    return (result.astype(jnp.bfloat16), loss, grads[0], grads[1], grads[2], grads[3], grads[4], grads[5], grads[6], grads[7], grads[8], grads[9], grads[10], grads[11], grads[12])
```

```python
import jax
import jax.numpy as jnp
from jax import lax
from jax.experimental import pallas as pl
from jax.experimental.pallas import tpu as pltpu
from jax.sharding import PartitionSpec as P

DH = 64
PIECE = 256
BLOCK = 256
LOCAL_HEADS = 3
HEAD_WIDTH = LOCAL_HEADS * DH
PAD = 256

norm_eps = 1e-06
masked_score = -1e30

bf16 = jnp.bfloat16
f32 = jnp.float32

CROSS_X = [(0, 1), (1, 0), (2, 3), (3, 2)]
CROSS_Y = [(0, 2), (2, 0), (1, 3), (3, 1)]
CROSS_ROW = [(0, 1), (1, 0)]


def send_x(a):
    return lax.ppermute(a, "col", CROSS_X)


def send_y(a):
    return lax.ppermute(a, "col", CROSS_Y)


def send_row(a):
    return lax.ppermute(a, "row", CROSS_ROW)


def send_dp(a, bit):
    size = lax.axis_size("dp")
    return lax.ppermute(a, "dp", [(i, i ^ bit) for i in range(size)])


def dot(a, b):
    return jnp.dot(a, b, preferred_element_type=f32)


def dot_nt(a, b):
    return lax.dot_general(a, b, (((1,), (1,)), ((), ())), preferred_element_type=f32)


def dot_tn(a, b):
    return lax.dot_general(a, b, (((0,), (0,)), ((), ())), preferred_element_type=f32)


def dp_bits():
    bits, bit = [], 1
    while bit < lax.axis_size("dp"):
        bits.append(bit)
        bit *= 2
    return bits


def sum_dp(part):
    if lax.axis_size("dp") != 4:
        return lax.psum(part.astype(bf16), "dp").astype(f32)
    place = lax.axis_index("dp")
    keep = part
    ups = []
    for bit in dp_bits():
        upper = (place // bit) % 2
        half = keep.shape[0] // 2
        mine = lax.dynamic_slice_in_dim(keep, upper * half, half)
        other = lax.dynamic_slice_in_dim(keep, (1 - upper) * half, half)
        keep = mine + send_dp(other.astype(bf16), bit).astype(f32)
        ups.append(upper)
    low = keep.astype(bf16)
    for bit, upper in zip(reversed(dp_bits()), reversed(ups)):
        came = send_dp(low, bit)
        low = jnp.where(
            upper == 0, jnp.concatenate([low, came]), jnp.concatenate([came, low])
        )
    return low.astype(f32)


def sum_dp_small(part):
    if lax.axis_size("dp") != 4:
        return lax.psum(part, "dp")
    for bit in dp_bits():
        part = part + send_dp(part, bit)
    return part


def norm_stats(values):
    center = jnp.mean(values, axis=1, keepdims=True)
    spread = jnp.mean(values * values, axis=1, keepdims=True) - center * center
    return center, lax.rsqrt(spread + norm_eps)


def head_stack(a):
    lane = lax.broadcasted_iota(jnp.int32, a.shape, 1)
    wide = a.astype(f32)
    parts = [
        jnp.where((lane >= h * DH) & (lane < (h + 1) * DH), wide, 0.0).astype(bf16)
        for h in range(LOCAL_HEADS)
    ]
    return jnp.concatenate(parts, axis=0)


def fill(half, own_ref, other_ref, scratch):
    rows = own_ref.shape[0]
    width = own_ref.shape[1]
    scratch[pl.ds(pl.multiple_of(half * rows, rows), rows), :width] = own_ref[...]
    scratch[pl.ds(pl.multiple_of((1 - half) * rows, rows), rows), :width] = other_ref[...]


def allowed_pair(kb, qb, key_ids, low_ref, high_ref):
    start = pl.multiple_of(kb * BLOCK, BLOCK)
    ids = key_ids[pl.ds(start, BLOCK), :]
    key_place = start + lax.broadcasted_iota(jnp.int32, (BLOCK, 1), 0)
    query_place = qb * BLOCK + lax.broadcasted_iota(jnp.int32, (1, BLOCK), 1)
    low = low_ref[pl.ds(qb, 1), :]
    high = high_ref[pl.ds(qb, 1), :]
    return ((ids >= low) & (ids <= high)) | (key_place == query_place)


def attend_kernel(
    meta, own_ref, other_ref, key_ids, low_ref, high_ref, out_ref, wide_ref, log_ref, qkv, values_t
):
    qb = pl.program_id(0)
    blocks = pl.num_programs(0)

    @pl.when(qb == 0)
    def _():
        fill(meta[0], own_ref, other_ref, qkv)
        for b in range(qkv.shape[0] // BLOCK):
            values_t[:, b * BLOCK : (b + 1) * BLOCK] = qkv[
                b * BLOCK : (b + 1) * BLOCK, 2 * PAD :
            ].T

    del blocks
    query = qkv[pl.ds(pl.multiple_of(qb * BLOCK, BLOCK), BLOCK), :PAD]
    stacked = head_stack(query.astype(f32) * DH ** (-0.5))

    def step(kb, carry):
        start = pl.multiple_of(kb * BLOCK, BLOCK)
        keys = qkv[pl.ds(start, BLOCK), PAD : 2 * PAD]
        scores = dot_nt(keys, stacked)
        allowed = allowed_pair(kb, qb, key_ids, low_ref, high_ref)
        new = []
        for h in range(LOCAL_HEADS):
            peak, total, mixed = carry[h]
            own = jnp.where(allowed, scores[:, h * BLOCK : (h + 1) * BLOCK], masked_score)
            peak_new = jnp.maximum(peak, jnp.max(own, axis=0, keepdims=True))
            weights = jnp.exp(own - peak_new)
            fade = jnp.exp(peak - peak_new)
            part = dot(
                values_t[h * DH : (h + 1) * DH, pl.ds(start, BLOCK)], weights.astype(bf16)
            )
            new.append(
                (peak_new, total * fade + jnp.sum(weights, axis=0, keepdims=True), mixed * fade + part)
            )
        return tuple(new)

    first = tuple(
        (
            jnp.full((1, BLOCK), masked_score, f32),
            jnp.zeros((1, BLOCK), f32),
            jnp.zeros((DH, BLOCK), f32),
        )
        for _ in range(LOCAL_HEADS)
    )
    done = lax.fori_loop(meta[1 + qb], qb + 1, step, first)
    for h in range(LOCAL_HEADS):
        peak, total, mixed = done[h]
        wide_ref[0, h * DH : (h + 1) * DH, :] = mixed / total
        log_ref[0, h : h + 1, :] = peak + jnp.log(total)
    out_ref[...] = wide_ref[0].T.astype(bf16)


def attend(meta, own, other, key_ids, low, high):
    length = 2 * own.shape[0]
    blocks = length // BLOCK
    half = blocks // 2

    def whole(shape):
        return pl.BlockSpec(shape, lambda i, m: (0,) * len(shape))

    return pl.pallas_call(
        attend_kernel,
        grid_spec=pltpu.PrefetchScalarGridSpec(
            num_scalar_prefetch=1,
            grid=(blocks,),
            in_specs=[
                whole(own.shape),
                whole(other.shape),
                whole(key_ids.shape),
                whole(low.shape),
                whole(high.shape),
            ],
            out_specs=[
                pl.BlockSpec((BLOCK, HEAD_WIDTH), lambda i, m: ((i + m[0] * half) % blocks, 0)),
                pl.BlockSpec((1, HEAD_WIDTH, BLOCK), lambda i, m: (i, 0, 0)),
                pl.BlockSpec((1, 8, BLOCK), lambda i, m: (i, 0, 0)),
            ],
            scratch_shapes=[
                pltpu.VMEM((length, 3 * PAD), bf16),
                pltpu.VMEM((PAD, length), bf16),
            ],
        ),
        out_shape=[
            jax.ShapeDtypeStruct((length, HEAD_WIDTH), bf16),
            jax.ShapeDtypeStruct((blocks, HEAD_WIDTH, BLOCK), f32),
            jax.ShapeDtypeStruct((blocks, 8, BLOCK), f32),
        ],
        name="attend",
    )(meta, own, other, key_ids, low, high)


def attend_back_kernel(
    meta,
    own_ref,
    other_ref,
    grad_own_ref,
    grad_other_ref,
    wide_ref,
    log_ref,
    key_ids,
    low_ref,
    high_ref,
    out_ref,
    qkv,
    grads,
    keys_t,
    key_grads,
    value_grads,
):
    qb = pl.program_id(0)
    blocks = pl.num_programs(0)
    length = qkv.shape[0]
    half_rows = length // 2

    @pl.when(qb == 0)
    def _():
        fill(meta[0], own_ref, other_ref, qkv)
        grads[...] = jnp.zeros_like(grads)
        fill(meta[0], grad_own_ref, grad_other_ref, grads)
        key_grads[...] = jnp.zeros_like(key_grads)
        value_grads[...] = jnp.zeros_like(value_grads)
        for b in range(length // BLOCK):
            keys_t[:, b * BLOCK : (b + 1) * BLOCK] = qkv[
                b * BLOCK : (b + 1) * BLOCK, PAD : 2 * PAD
            ].T

    rows = pl.ds(pl.multiple_of(qb * BLOCK, BLOCK), BLOCK)
    stacked = head_stack(qkv[rows, :PAD].astype(f32) * DH ** (-0.5))
    grad = grads[rows, :]
    grad_stacked = head_stack(grad)
    product = grad.astype(f32).T[:HEAD_WIDTH] * wide_ref[0]
    deltas = [
        jnp.sum(product[h * DH : (h + 1) * DH], axis=0, keepdims=True) for h in range(LOCAL_HEADS)
    ]
    logs = [log_ref[0, h : h + 1, :] for h in range(LOCAL_HEADS)]

    def step(kb, carry):
        start = pl.multiple_of(kb * BLOCK, BLOCK)
        here = pl.ds(start, BLOCK)
        keys = qkv[here, PAD : 2 * PAD]
        values = qkv[here, 2 * PAD :]
        scores = dot_nt(keys, stacked)
        grad_probs = dot_nt(values, grad_stacked)
        allowed = allowed_pair(kb, qb, key_ids, low_ref, high_ref)
        probs_all, grads_all, new = [], [], []
        for h in range(LOCAL_HEADS):
            span = slice(h * BLOCK, (h + 1) * BLOCK)
            probs = jnp.exp(jnp.where(allowed, scores[:, span], masked_score) - logs[h])
            grad_scores = (probs * (grad_probs[:, span] - deltas[h])).astype(bf16)
            probs_all.append(probs.astype(bf16))
            grads_all.append(grad_scores)
            new.append(carry[h] + dot(keys_t[h * DH : (h + 1) * DH, here], grad_scores))
        value_grads[here, :] += dot(jnp.concatenate(probs_all, axis=1), grad_stacked)
        key_grads[here, :] += dot(jnp.concatenate(grads_all, axis=1), stacked)
        return tuple(new)

    query_grads = lax.fori_loop(
        meta[1 + qb],
        qb + 1,
        step,
        tuple(jnp.zeros((DH, BLOCK), f32) for _ in range(LOCAL_HEADS)),
    )
    local = (qb + meta[0] * (blocks // 2)) % blocks
    spread = jnp.concatenate(list(query_grads) + [jnp.zeros((PAD - HEAD_WIDTH, BLOCK), f32)], axis=0)
    out_ref[pl.ds(pl.multiple_of(local * BLOCK, BLOCK), BLOCK), :PAD] = (
        spread.T * DH ** (-0.5)
    ).astype(bf16)

    @pl.when(qb == blocks - 1)
    def _():
        mine = pl.ds(pl.multiple_of(meta[0] * half_rows, half_rows), half_rows)
        theirs = pl.ds(pl.multiple_of((1 - meta[0]) * half_rows, half_rows), half_rows)
        for at, total in ((PAD, key_grads), (2 * PAD, value_grads)):
            out_ref[:half_rows, at : at + PAD] = total[mine, :].astype(bf16)
            out_ref[half_rows:, at : at + PAD] = total[theirs, :].astype(bf16)


def attend_back(meta, own, other, grad_own, grad_other, wide, log, key_ids, low, high):
    length = 2 * own.shape[0]
    blocks = length // BLOCK

    def whole(shape):
        return pl.BlockSpec(shape, lambda i, m: (0,) * len(shape))

    return pl.pallas_call(
        attend_back_kernel,
        grid_spec=pltpu.PrefetchScalarGridSpec(
            num_scalar_prefetch=1,
            grid=(blocks,),
            in_specs=[
                whole(own.shape),
                whole(other.shape),
                whole(grad_own.shape),
                whole(grad_other.shape),
                pl.BlockSpec((1, HEAD_WIDTH, BLOCK), lambda i, m: (i, 0, 0)),
                pl.BlockSpec((1, 8, BLOCK), lambda i, m: (i, 0, 0)),
                whole(key_ids.shape),
                whole(low.shape),
                whole(high.shape),
            ],
            out_specs=whole((length, 3 * PAD)),
            scratch_shapes=[
                pltpu.VMEM((length, 3 * PAD), bf16),
                pltpu.VMEM((length, PAD), bf16),
                pltpu.VMEM((PAD, length), bf16),
                pltpu.VMEM((length, PAD), f32),
                pltpu.VMEM((length, PAD), f32),
            ],
        ),
        out_shape=jax.ShapeDtypeStruct((length, 3 * PAD), bf16),
        name="attend_back",
    )(meta, own, other, grad_own, grad_other, wide, log, key_ids, low, high)


def both_halves(own, axis=0):
    return jnp.concatenate([own, send_row(own)], axis=axis)


def on_device(
    states,
    teacher,
    valid_mask,
    seg_ids,
    piece_start,
    norm1_gain,
    norm1_bias,
    w_qkv,
    b_qv,
    w_out,
    b_out,
    norm2_gain,
    norm2_bias,
    w_up,
    b_up,
    w_down,
    b_down,
):
    row = lax.axis_index("row")
    col = lax.axis_index("col")
    half = col % 2
    first = row == 0
    chip_tokens, half_width = states.shape
    tokens = chip_tokens // lax.axis_size("row")
    width = half_width * lax.axis_size("row")
    length = seg_ids.shape[1]
    all_tokens = valid_mask.shape[0] * lax.axis_size("dp")
    blocks = length // BLOCK

    def own_rows(a):
        return lax.dynamic_slice_in_dim(a, row * tokens, tokens)

    def mate_rows(a):
        return lax.dynamic_slice_in_dim(a, (1 - row) * tokens, tokens)

    states_x = send_x(states)
    states_mate = send_row(states)
    states_x_mate = send_row(states_x)

    tables = jnp.concatenate([seg_ids, piece_start], axis=0)
    tables = jnp.where(row == col // 2, tables, send_row(tables))
    segs, starts = tables[0], tables[1]
    mask_row = lax.dynamic_slice_in_dim(valid_mask, (col // 2) * length, length)
    places = jnp.arange(length, dtype=jnp.int32)
    ends = [jnp.sum((segs <= s).astype(jnp.int32)) for s in range(3)]
    low = jnp.where(
        segs == 0, 0, jnp.where(segs == 1, ends[0], jnp.where(segs == 2, ends[1], ends[2]))
    )
    high = jnp.where(
        segs == 0, ends[0], jnp.where(segs == 1, ends[1], jnp.where(segs == 2, ends[2], length))
    )
    high = jnp.minimum(high - 1, jnp.maximum(places, starts + PIECE - 1))
    key_ids = jnp.where(mask_row > 0, places, -1)[:, None]
    low_rows = low.reshape(blocks, BLOCK)
    high_rows = high.reshape(blocks, BLOCK)
    meta = jnp.concatenate([half[None].astype(jnp.int32), low_rows[:, 0] // BLOCK])

    small = both_halves(
        jnp.stack([norm1_gain, norm1_bias, norm2_gain, norm2_bias, b_out, b_down]), axis=1
    )
    gain1, shift1, gain2, shift2, bias_out, bias_down = (small[i][None, :] for i in range(6))
    count = sum_dp_small(jnp.broadcast_to(jnp.sum(valid_mask.astype(f32)), (8, 128)))[0, 0]

    w_qkv_flat = w_qkv.reshape(half_width, 3 * HEAD_WIDTH)
    qkv_y = send_y(w_qkv_flat)
    qkv_own = jnp.where(first, w_qkv_flat, qkv_y)
    qkv_mate = send_row(jnp.where(first, qkv_y, w_qkv_flat))
    qkv_matrix = jnp.concatenate([qkv_own, qkv_mate], axis=0).reshape(width, 3, HEAD_WIDTH)
    qkv_matrix = jnp.pad(qkv_matrix, ((0, 0), (0, 0), (0, PAD - HEAD_WIDTH))).reshape(width, 3 * PAD)
    qv_y = send_y(b_qv)
    qv_own = jnp.where(first, b_qv, qv_y)
    qv_pad = jnp.pad(qv_own, ((0, 0), (0, PAD - HEAD_WIDTH)))
    qkv_bias = jnp.concatenate([qv_pad[0], jnp.zeros((PAD,), f32), qv_pad[1]])[None, :]

    def gather_blocks(own):
        over_x = send_x(own)
        over_y = send_y(own)
        return [own, over_x, over_y, send_y(over_x)]

    out_own = jnp.concatenate(gather_blocks(w_out), axis=0)
    out_matrix = both_halves(out_own, axis=1)
    up_own = jnp.concatenate(gather_blocks(w_up), axis=1)
    up_matrix = both_halves(up_own, axis=0)
    up_bias = jnp.concatenate(gather_blocks(b_up[None, :]), axis=1)
    down_own = jnp.concatenate(gather_blocks(w_down), axis=0)
    down_matrix = both_halves(down_own, axis=1)

    def project(left, right):
        values = jnp.concatenate([left, right], axis=1).astype(f32)
        center, inverse = norm_stats(values)
        hidden = ((values - center) * inverse * gain1 + shift1).astype(bf16)
        return hidden, (dot(hidden, qkv_matrix) + qkv_bias).astype(bf16), center, inverse

    hidden_own, qkv_own_rows, center_own, inverse_own = project(states, states_mate)
    hidden_x, qkv_x_rows, center_x, inverse_x = project(states_x, states_x_mate)

    attended, wide, log = attend(meta, qkv_own_rows, qkv_x_rows, key_ids, low_rows, high_rows)
    pair = jnp.concatenate([attended[:chip_tokens], send_x(attended[chip_tokens:])], axis=1)
    mine = own_rows(pair)
    came = send_row(mate_rows(pair))
    attended_rows = jnp.concatenate(
        [jnp.where(first, mine, came), jnp.where(first, came, mine)], axis=1
    )

    state_rows = jnp.concatenate([own_rows(states), own_rows(states_mate)], axis=1).astype(f32)
    middle = state_rows + dot(attended_rows, out_matrix) + bias_out
    center2, inverse2 = norm_stats(middle)
    normed2 = (middle - center2) * inverse2
    hidden2 = (normed2 * gain2 + shift2).astype(bf16)
    upper = dot(hidden2, up_matrix) + up_bias
    cdf = 0.5 * (1.0 + lax.erf(upper * (0.5**0.5)))
    act = (upper * cdf).astype(bf16)
    result = middle + dot(act, down_matrix) + bias_down

    teacher_mate = send_row(mate_rows(teacher))
    teacher_rows = jnp.concatenate([own_rows(teacher), teacher_mate], axis=1).astype(f32)
    valid_rows = lax.dynamic_slice_in_dim(
        valid_mask, col * chip_tokens + row * tokens, tokens
    ).astype(f32)
    diff = (result - teacher_rows) * valid_rows[:, None]
    loss_part = jnp.sum(diff * diff)
    grad_result = diff * (all_tokens / count)
    grad_low = grad_result.astype(bf16)

    def to_chip_rows(own_half, other_half):
        came = send_row(other_half)
        return jnp.where(
            first,
            jnp.concatenate([own_half, came], axis=0),
            jnp.concatenate([came, own_half], axis=0),
        )

    result_low = result.astype(bf16)
    out = to_chip_rows(result_low[:, :half_width], result_low[:, half_width:])

    def reduce_rows_of(part, axis):
        keep = lax.slice_in_dim(part, 0, half_width, axis=axis)
        give = lax.slice_in_dim(part, half_width, width, axis=axis)
        return keep + send_row(give.astype(bf16)).astype(f32)

    def reduce_blocks(part, axis):
        size = part.shape[axis] // 4
        near = lax.slice_in_dim(part, 0, 2 * size, axis=axis)
        far = lax.slice_in_dim(part, 2 * size, 4 * size, axis=axis)
        near = near + send_y(far.astype(bf16)).astype(f32)
        keep = lax.slice_in_dim(near, 0, size, axis=axis)
        give = lax.slice_in_dim(near, size, 2 * size, axis=axis)
        return keep + send_x(give.astype(bf16)).astype(f32)

    grad_w_down = sum_dp(reduce_blocks(reduce_rows_of(dot_tn(act, grad_low), 1), 0))
    grad_act = dot_nt(grad_low, down_matrix)
    density = jnp.exp(-0.5 * upper * upper) * 0.3989422804014327
    grad_upper = (grad_act * (cdf + upper * density)).astype(bf16)
    grad_w_up = sum_dp(reduce_blocks(reduce_rows_of(dot_tn(hidden2, grad_upper), 0), 1))
    grad_hidden2 = dot_nt(grad_upper, up_matrix)

    scaled2 = grad_hidden2 * gain2
    grad_middle = grad_result + inverse2 * (
        scaled2
        - jnp.mean(scaled2, axis=1, keepdims=True)
        - normed2 * jnp.mean(scaled2 * normed2, axis=1, keepdims=True)
    )
    middle_low = grad_middle.astype(bf16)
    grad_w_out = sum_dp(reduce_blocks(reduce_rows_of(dot_tn(attended_rows, middle_low), 1), 0))
    grad_attended = dot_nt(middle_low, out_matrix).astype(bf16)

    near = grad_attended[:, : 2 * HEAD_WIDTH]
    far = grad_attended[:, 2 * HEAD_WIDTH :]
    keep = jnp.where(first, near, far)
    came = send_row(jnp.where(first, far, near))
    pair = jnp.where(
        first, jnp.concatenate([keep, came], axis=0), jnp.concatenate([came, keep], axis=0)
    )
    grad_own = pair[:, :HEAD_WIDTH]
    grad_x_rows = send_x(pair[:, HEAD_WIDTH:])
    grad_qkv = attend_back(
        meta,
        qkv_own_rows,
        qkv_x_rows,
        grad_own,
        grad_x_rows,
        wide,
        log,
        key_ids,
        low_rows,
        high_rows,
    )
    grad_hidden1 = dot_nt(grad_qkv, qkv_matrix)
    part_qkv = dot_tn(jnp.concatenate([hidden_own, hidden_x], axis=0), grad_qkv)
    part_qkv = part_qkv.reshape(width, 3, PAD)[:, :, :HEAD_WIDTH].reshape(width, 3 * HEAD_WIDTH)

    own_half, other_half = part_qkv[:half_width], part_qkv[half_width:]
    came = send_row(other_half.astype(bf16)).astype(f32)
    stays = jnp.where(first, own_half, came)
    goes = jnp.where(first, came, own_half)
    grad_w_qkv = sum_dp(stays + send_y(goes.astype(bf16)).astype(f32)).reshape(w_qkv.shape)

    def norm1_values(left, right, center, inverse):
        values = jnp.concatenate([left, right], axis=1).astype(f32)
        return (values - center) * inverse

    normed1_own = norm1_values(states, states_mate, center_own, inverse_own)
    normed1_x = norm1_values(states_x, states_x_mate, center_x, inverse_x)
    normed1 = jnp.concatenate([normed1_own, normed1_x], axis=0)
    scaled1 = grad_hidden1 * gain1
    sums = jnp.stack([jnp.sum(scaled1, axis=1), jnp.sum(scaled1 * normed1, axis=1)])
    sums = sums + send_row(sums)
    sums = sums[:, :chip_tokens] + send_x(sums[:, chip_tokens:])
    sums = sums / width
    gain1_part = jnp.sum(grad_hidden1 * normed1, axis=0)
    shift1_part = jnp.sum(grad_hidden1, axis=0)
    reduced = reduce_rows_of(grad_hidden1, 1)
    reduced = reduced[:chip_tokens] + send_x(reduced[chip_tokens:].astype(bf16)).astype(f32)
    middle_chip = to_chip_rows(grad_middle[:, :half_width], grad_middle[:, half_width:])
    grad_x = middle_chip + inverse_own * (
        reduced * gain1[:, :half_width]
        - sums[0][:, None]
        - normed1_own[:, :half_width] * sums[1][:, None]
    )

    features = jnp.stack(
        [
            jnp.sum(grad_hidden2 * normed2, axis=0),
            jnp.sum(grad_hidden2, axis=0),
            jnp.sum(middle_low.astype(f32), axis=0),
            jnp.sum(grad_low.astype(f32), axis=0),
        ]
    )
    grad_b_up = jnp.sum(grad_upper.astype(f32), axis=0)
    loss_row = jnp.broadcast_to(loss_part, (1, half_width))
    keep = jnp.concatenate(
        [features[:, :half_width], loss_row, grad_b_up.reshape(8, half_width)], axis=0
    )
    give = jnp.concatenate([features[:, half_width:], keep[4:]], axis=0)
    total = keep + send_row(give)
    far = total[9:]
    total = total[:9] + send_y(jnp.concatenate([total[:5], far], axis=0))
    total = total[:7] + send_x(jnp.concatenate([total[:5], total[7:]], axis=0))
    total = sum_dp_small(total)
    grad_norm2_gain, grad_norm2_bias, grad_b_out, grad_b_down = (total[i] for i in range(4))
    loss = total[4, 0] / (count * width)
    grad_b_up = total[5:7].reshape(b_up.shape)

    column_sums = jnp.sum(grad_qkv.astype(f32), axis=0).reshape(3, PAD)[:, :HEAD_WIDTH]
    late = jnp.stack([gain1_part, shift1_part]).reshape(2, 2, half_width)
    mine_qv = jnp.concatenate([column_sums[0], column_sums[2]])[None, :]
    early = jnp.concatenate([late[:, 0], late[:, 1], mine_qv], axis=0)
    over_y = send_y(early)
    qv = jnp.where(first, mine_qv, over_y[4:])
    features = early[:4] + over_y[:4]
    over_row = send_row(jnp.concatenate([features[2:], qv], axis=0))
    features = features[:2] + over_row[:2]
    qv = qv + over_row[2:]
    features = features + send_x(features)
    late = sum_dp_small(jnp.concatenate([features, qv], axis=0))
    grad_norm1_gain, grad_norm1_bias = late[0], late[1]
    grad_b_qv = late[2].reshape(b_qv.shape)

    return (
        out,
        loss,
        grad_x,
        grad_norm1_gain,
        grad_norm1_bias,
        grad_w_qkv,
        grad_b_qv,
        grad_w_out,
        grad_b_out,
        grad_norm2_gain,
        grad_norm2_bias,
        grad_w_up,
        grad_b_up,
        grad_w_down,
        grad_b_down,
    )


def solution(mesh):
    placed = (
        P(("dp", "col"), "row"),
        P(("dp", "col"), "row"),
        P("dp"),
        P(("dp", "row"), None),
        P(("dp", "row"), None),
        P("row"),
        P("row"),
        P("row", None, "col"),
        P(None, "col"),
        P("col", "row"),
        P("row"),
        P("row"),
        P("row"),
        P("row", "col"),
        P("col"),
        P("col", "row"),
        P("row"),
    )
    return jax.shard_map(
        on_device,
        mesh=mesh,
        in_specs=placed,
        out_specs=(
            P(("dp", "col"), "row"),
            P(),
            P(("dp", "col"), "row"),
            P("row"),
            P("row"),
            P("row", None, "col"),
            P(None, "col"),
            P("col", "row"),
            P("row"),
            P("row"),
            P("row"),
            P("row", "col"),
            P("col"),
            P("col", "row"),
            P("row"),
        ),
        check_vma=False,
    )
```

```python
import jax
import jax.numpy as jnp
from jax import lax
from jax.experimental import pallas as pl
from jax.experimental.pallas import tpu as pltpu
from jax.sharding import PartitionSpec as P

DH = 64
PIECE = 256
BLOCK = 256
LOCAL_HEADS = 3
HEAD_WIDTH = LOCAL_HEADS * DH
PAD = 256

norm_eps = 1e-06
masked_score = -1e30


bf16 = jnp.bfloat16
f32 = jnp.float32

CROSS_X = [(0, 1), (1, 0), (2, 3), (3, 2)]
CROSS_Y = [(0, 2), (2, 0), (1, 3), (3, 1)]
CROSS_ROW = [(0, 1), (1, 0)]


def send_x(a):
    return lax.ppermute(a, "col", CROSS_X)


def send_y(a):
    return lax.ppermute(a, "col", CROSS_Y)


def send_row(a):
    return lax.ppermute(a, "row", CROSS_ROW)


def send_dp(a, bit):
    size = lax.axis_size("dp")
    return lax.ppermute(a, "dp", [(i, i ^ bit) for i in range(size)])


def dot(a, b):
    return jnp.dot(a, b, preferred_element_type=f32)


def dot_nt(a, b):
    return lax.dot_general(a, b, (((1,), (1,)), ((), ())), preferred_element_type=f32)


def dot_tn(a, b):
    return lax.dot_general(a, b, (((0,), (0,)), ((), ())), preferred_element_type=f32)


def dp_bits():
    bits, bit = [], 1
    while bit < lax.axis_size("dp"):
        bits.append(bit)
        bit *= 2
    return bits


def sum_dp(part):
    if lax.axis_size("dp") != 4:
        return lax.psum(part.astype(bf16), "dp").astype(f32)
    place = lax.axis_index("dp")
    keep = part
    ups = []
    for bit in dp_bits():
        upper = (place // bit) % 2
        half = keep.shape[0] // 2
        mine = lax.dynamic_slice_in_dim(keep, upper * half, half)
        other = lax.dynamic_slice_in_dim(keep, (1 - upper) * half, half)
        keep = mine + send_dp(other.astype(bf16), bit).astype(f32)
        ups.append(upper)
    low = keep.astype(bf16)
    for bit, upper in zip(reversed(dp_bits()), reversed(ups)):
        came = send_dp(low, bit)
        low = jnp.where(
            upper == 0, jnp.concatenate([low, came]), jnp.concatenate([came, low])
        )
    return low.astype(f32)


def sum_dp_small(part):
    if lax.axis_size("dp") != 4:
        return lax.psum(part, "dp")
    for bit in dp_bits():
        part = part + send_dp(part, bit)
    return part


def norm_stats(values):
    center = jnp.mean(values, axis=1, keepdims=True)
    spread = jnp.mean(values * values, axis=1, keepdims=True) - center * center
    return center, lax.rsqrt(spread + norm_eps)


def head_stack(a):
    lane = lax.broadcasted_iota(jnp.int32, a.shape, 1)
    wide = a.astype(f32)
    parts = [
        jnp.where((lane >= h * DH) & (lane < (h + 1) * DH), wide, 0.0).astype(bf16)
        for h in range(LOCAL_HEADS)
    ]
    return jnp.concatenate(parts, axis=0)


def span(at, size):
    return pl.ds(pl.multiple_of(at, size), size)


def call(kernel, name, outs, scratch=(), smem=(), hbm=(), aliases=None):
    def run(*args):
        specs = []
        for i in range(len(args)):
            if i in smem:
                specs.append(pl.BlockSpec(memory_space=pltpu.SMEM))
            elif i in hbm:
                specs.append(pl.BlockSpec(memory_space=pl.ANY))
            else:
                specs.append(pl.BlockSpec(memory_space=pltpu.VMEM))
        return pl.pallas_call(
            kernel,
            in_specs=specs,
            out_specs=[pl.BlockSpec(memory_space=pltpu.VMEM) for _ in outs],
            out_shape=[jax.ShapeDtypeStruct(*o) for o in outs],
            scratch_shapes=list(scratch),
            name=name,
        )(*args)

    return run


def project_kernel(left, right, gain, shift, weights, bias, hidden_ref, qkv_ref):
    rows = 256

    def step(i, _):
        at = span(i * rows, rows)
        values = jnp.concatenate([left[at, :], right[at, :]], axis=1).astype(f32)
        center, inverse = norm_stats(values)
        hidden = ((values - center) * inverse * gain[...] + shift[...]).astype(bf16)
        hidden_ref[at, :] = hidden
        qkv_ref[at, :] = (dot(hidden, weights[...]) + bias[...]).astype(bf16)
        return 0

    lax.fori_loop(0, left.shape[0] // rows, step, 0)


def project(left, right, gain, shift, weights, bias):
    rows = left.shape[0]
    return call(
        project_kernel,
        "project",
        [((rows, weights.shape[0]), bf16), ((rows, weights.shape[1]), bf16)],
    )(left, right, gain, shift, weights, bias)


def fill(half, own_ref, other_ref, scratch):
    rows, width = own_ref.shape
    scratch[span(half * rows, rows), :width] = own_ref[...]
    scratch[span((1 - half) * rows, rows), :width] = other_ref[...]


def allowed_pair(kb, qb, key_ids, low_ref, high_ref):
    start = pl.multiple_of(kb * BLOCK, BLOCK)
    ids = key_ids[pl.ds(start, BLOCK), :]
    key_place = start + lax.broadcasted_iota(jnp.int32, (BLOCK, 1), 0)
    query_place = qb * BLOCK + lax.broadcasted_iota(jnp.int32, (1, BLOCK), 1)
    low = low_ref[pl.ds(qb, 1), :]
    high = high_ref[pl.ds(qb, 1), :]
    return ((ids >= low) & (ids <= high)) | (key_place == query_place)


def attend_kernel(
    meta, own_ref, other_ref, key_ids, low_ref, high_ref, out_ref, wide_ref, log_ref, qkv, values_t
):
    fill(meta[0], own_ref, other_ref, qkv)
    length = qkv.shape[0]
    for b in range(length // BLOCK):
        at = slice(b * BLOCK, (b + 1) * BLOCK)
        values_t[:, at] = qkv[at, 2 * PAD :].T
    count = wide_ref.shape[0]
    base = meta[1] * count

    def block(i, _):
        qb = base + i
        stacked = head_stack(qkv[span(qb * BLOCK, BLOCK), :PAD].astype(f32) * DH ** (-0.5))

        def step(kb, carry):
            at = span(kb * BLOCK, BLOCK)
            scores = dot_nt(qkv[at, PAD : 2 * PAD], stacked)
            allowed = allowed_pair(kb, qb, key_ids, low_ref, high_ref)
            new = []
            for h in range(LOCAL_HEADS):
                peak, total, mixed = carry[h]
                own = jnp.where(allowed, scores[:, h * BLOCK : (h + 1) * BLOCK], masked_score)
                peak_new = jnp.maximum(peak, jnp.max(own, axis=0, keepdims=True))
                weights = jnp.exp(own - peak_new)
                fade = jnp.exp(peak - peak_new)
                part = dot(values_t[h * DH : (h + 1) * DH, at], weights.astype(bf16))
                total = total * fade + jnp.sum(weights, axis=0, keepdims=True)
                new.append((peak_new, total, mixed * fade + part))
            return tuple(new)

        first = tuple(
            (
                jnp.full((1, BLOCK), masked_score, f32),
                jnp.zeros((1, BLOCK), f32),
                jnp.zeros((DH, BLOCK), f32),
            )
            for _ in range(LOCAL_HEADS)
        )
        done = lax.fori_loop(meta[2 + qb], qb + 1, step, first)
        mixes = []
        for h in range(LOCAL_HEADS):
            peak, total, mixed = done[h]
            mixes.append(mixed / total)
            log_ref[i, h : h + 1, :] = peak + jnp.log(total)
        wide = jnp.concatenate(mixes, axis=0)
        wide_ref[i] = wide
        out_ref[span(i * BLOCK, BLOCK), :] = wide.T.astype(bf16)
        return 0

    lax.fori_loop(0, count, block, 0)


def attend(meta, own, other, key_ids, low, high):
    rows = own.shape[0]
    count = rows // BLOCK
    return call(
        attend_kernel,
        "attend",
        [((rows, HEAD_WIDTH), bf16), ((count, HEAD_WIDTH, BLOCK), f32), ((count, 8, BLOCK), f32)],
        scratch=[pltpu.VMEM((2 * rows, 3 * PAD), bf16), pltpu.VMEM((PAD, 2 * rows), bf16)],
        smem=(0,),
    )(meta, own, other, key_ids, low, high)


def attend_back_kernel(last, *refs):
    (meta, own_ref, other_ref, grad_a, grad_b, wide_ref, log_ref, key_ids, low_ref, high_ref) = refs[
        :10
    ]
    if last:
        key_in, value_in, out_own, out_other, query_in, qkv, keys_t, key_grads, value_grads = (
            refs[10],
            refs[11],
            refs[13],
            refs[14],
            refs[12],
            refs[15],
            refs[16],
            refs[17],
            refs[18],
        )
    else:
        out_query, key_grads, value_grads, qkv, keys_t = refs[10:]
    half = meta[0]
    length = qkv.shape[0]
    rows = length // 2
    small = rows // 2
    fill(half, own_ref, other_ref, qkv)
    for b in range(length // BLOCK):
        at = slice(b * BLOCK, (b + 1) * BLOCK)
        keys_t[:, at] = qkv[at, PAD : 2 * PAD].T
    if last:
        key_grads[...] = key_in[...]
        value_grads[...] = value_in[...]
    else:
        key_grads[...] = jnp.zeros_like(key_grads)
        value_grads[...] = jnp.zeros_like(value_grads)
    count = wide_ref.shape[0]
    base = meta[1] * count
    blank = jnp.zeros((BLOCK, PAD - HEAD_WIDTH), bf16)

    def block(i, _):
        qb = base + i
        stacked = head_stack(qkv[span(qb * BLOCK, BLOCK), :PAD].astype(f32) * DH ** (-0.5))
        inner = span((i % (small // BLOCK)) * BLOCK, BLOCK)
        mine = (i // (small // BLOCK)) == meta[2]
        grad = jnp.where(mine, grad_a[inner, :].astype(f32), grad_b[inner, :].astype(f32))
        grad = jnp.concatenate([grad.astype(bf16), blank], axis=1)
        grad_stacked = head_stack(grad)
        product = grad.astype(f32).T[:HEAD_WIDTH] * wide_ref[i]
        deltas = [
            jnp.sum(product[h * DH : (h + 1) * DH], axis=0, keepdims=True)
            for h in range(LOCAL_HEADS)
        ]
        logs = [log_ref[i, h : h + 1, :] for h in range(LOCAL_HEADS)]

        def step(kb, carry):
            at = span(kb * BLOCK, BLOCK)
            scores = dot_nt(qkv[at, PAD : 2 * PAD], stacked)
            grad_probs = dot_nt(qkv[at, 2 * PAD :], grad_stacked)
            allowed = allowed_pair(kb, qb, key_ids, low_ref, high_ref)
            probs_all, grads_all, new = [], [], []
            for h in range(LOCAL_HEADS):
                lanes = slice(h * BLOCK, (h + 1) * BLOCK)
                probs = jnp.exp(jnp.where(allowed, scores[:, lanes], masked_score) - logs[h])
                grad_scores = (probs * (grad_probs[:, lanes] - deltas[h])).astype(bf16)
                probs_all.append(probs.astype(bf16))
                grads_all.append(grad_scores)
                new.append(carry[h] + dot(keys_t[h * DH : (h + 1) * DH, at], grad_scores))
            value_grads[at, :] += dot(jnp.concatenate(probs_all, axis=1), grad_stacked)
            key_grads[at, :] += dot(jnp.concatenate(grads_all, axis=1), stacked)
            return tuple(new)

        grads = lax.fori_loop(
            meta[3 + qb],
            qb + 1,
            step,
            tuple(jnp.zeros((DH, BLOCK), f32) for _ in range(LOCAL_HEADS)),
        )
        wide = jnp.concatenate(list(grads) + [jnp.zeros((PAD - HEAD_WIDTH, BLOCK), f32)], axis=0)
        query = (wide.T * DH ** (-0.5)).astype(bf16)
        if last:
            out_other[span(i * BLOCK, BLOCK), :PAD] = query
        else:
            out_query[span(i * BLOCK, BLOCK), :] = query
        return 0

    lax.fori_loop(0, count, block, 0)
    if last:
        out_own[:, :PAD] = query_in[...]
        for at, total in ((PAD, key_grads), (2 * PAD, value_grads)):
            out_own[:, at : at + PAD] = total[span(half * rows, rows), :].astype(bf16)
            out_other[:, at : at + PAD] = total[span((1 - half) * rows, rows), :].astype(bf16)


def attend_back(meta, own, other, grad_a, grad_b, wide, log, key_ids, low, high, sums=None):
    rows = own.shape[0]
    length = 2 * rows
    last = sums is not None

    def kernel(*refs):
        attend_back_kernel(last, *refs)

    scratch = [pltpu.VMEM((length, 3 * PAD), bf16), pltpu.VMEM((PAD, length), bf16)]
    if last:
        scratch += [pltpu.VMEM((length, PAD), f32), pltpu.VMEM((length, PAD), f32)]
        outs = [((rows, 3 * PAD), bf16), ((rows, 3 * PAD), bf16)]
    else:
        outs = [((rows, PAD), bf16), ((length, PAD), f32), ((length, PAD), f32)]
    return call(
        kernel, "attend_back_last" if last else "attend_back_first", outs, scratch=scratch, smem=(0,)
    )(meta, own, other, grad_a, grad_b, wide, log, key_ids, low, high, *(sums or ()))


UP_ROWS = 384
OUT_ROWS = 96
PACK_ROWS = UP_ROWS + OUT_ROWS + 16


def pack_up(w_up, w_out, b_up):
    high = b_up.astype(bf16)
    low = (b_up - high.astype(f32)).astype(bf16)
    out_rows = jnp.concatenate([w_out[:OUT_ROWS], w_out[OUT_ROWS:]], axis=1)
    bias = jnp.stack([high, low])
    return jnp.concatenate([w_up, out_rows, jnp.pad(bias, ((0, 14), (0, 0)))], axis=0)


def copies_of_packs(packs, mates, up, out, bias, sems):
    todo = []
    half = up.shape[1] // 2

    def add(src, dst):
        todo.append(pltpu.make_async_copy(src, dst, sems.at[len(todo)]))

    for b in range(4):
        for k, source in enumerate((packs[b], mates[b])):
            lanes = pl.ds(k * half, half)
            for part in range(2):
                add(
                    source.at[pl.ds(UP_ROWS, OUT_ROWS), pl.ds(part * half, half)],
                    out.at[pl.ds(b * 2 * OUT_ROWS + part * OUT_ROWS, OUT_ROWS), lanes],
                )
            add(source.at[pl.ds(0, UP_ROWS), :], up.at[b, lanes, :])
        if bias is not None:
            add(packs[b].at[pl.ds(UP_ROWS + OUT_ROWS, 16), :], bias.at[b])
    return todo


def lift_kernel(*refs):
    (row, near_a, near_b, far_a, far_b, left, right, bias_out, gain, shift) = refs[:10]
    packs, mates = refs[10:14], refs[14:18]
    middle_ref, hidden_ref, act_ref, slope_ref, chip_ref = refs[18:23]
    up, out, bias, sems = refs[23:]
    todo = copies_of_packs(packs, mates, up, out, bias, sems)
    for c in todo:
        c.start()
    @pl.when(row[0] == 0)
    def _():
        for at, piece in enumerate((near_a, near_b, far_a, far_b)):
            chip_ref[:, at * HEAD_WIDTH : (at + 1) * HEAD_WIDTH] = piece[...]

    @pl.when(row[0] == 1)
    def _():
        for at, piece in enumerate((far_a, far_b, near_a, near_b)):
            chip_ref[:, at * HEAD_WIDTH : (at + 1) * HEAD_WIDTH] = piece[...]

    tokens = middle_ref.shape[0]
    tile = 256
    for c in todo:
        c.wait()

    def head(i, _):
        at = span(i * tile, tile)
        there = span(row[0] * tokens + i * tile, tile)
        values = jnp.concatenate([left[there, :], right[there, :]], axis=1).astype(f32)
        middle = values + dot(chip_ref[there, :], out[...]) + bias_out[...]
        middle_ref[at, :] = middle
        center, inverse = norm_stats(middle)
        hidden_ref[at, :] = ((middle - center) * inverse * gain[...] + shift[...]).astype(bf16)
        return 0

    lax.fori_loop(0, tokens // tile, head, 0)
    small = 128

    def body(n, _):
        b = n // (tokens // small)
        at = span((n % (tokens // small)) * small, small)
        line = bias[b, 0:1, :].astype(f32) + bias[b, 1:2, :].astype(f32)
        upper = dot(hidden_ref[at, :], up[b]) + line
        cdf = 0.5 * (1.0 + lax.erf(upper * (0.5**0.5)))
        act_ref[b, at, :] = (upper * cdf).astype(bf16)
        density = jnp.exp(-0.5 * upper * upper) * 0.3989422804014327
        slope_ref[b, at, :] = (cdf + upper * density).astype(bf16)
        return 0

    lax.fori_loop(0, 4 * (tokens // small), body, 0)


def lift(row, pieces, left, right, bias_out, gain, shift, packs, mates):
    chip, half = left.shape
    tokens, width = chip // 2, 2 * half
    return call(
        lift_kernel,
        "lift",
        [
            ((tokens, width), f32),
            ((tokens, width), bf16),
            ((4, tokens, width), bf16),
            ((4, tokens, width), bf16),
            ((chip, width), bf16),
        ],
        scratch=[
            pltpu.VMEM((4, width, width), bf16),
            pltpu.VMEM((width, width), bf16),
            pltpu.VMEM((4, 16, width), bf16),
            pltpu.SemaphoreType.DMA((28,)),
        ],
        smem=(0,),
        hbm=tuple(range(10, 18)),
    )(row, *pieces, left, right, bias_out, gain, shift, *packs, *mates)


def drop_kernel(*refs):
    (row, scale, act, slope, middle, bias, teach_own, teach_mate, valid) = refs[:9]
    own, mates = refs[9:13], refs[13:17]
    out_own, out_mate, grad_ref, low_own, low_mate, upper_ref, loss_ref = refs[17:24]
    down, sems = refs[24:]
    half = low_own.shape[1]
    todo = []
    for b in range(4):
        for k, source in enumerate((own[b], mates[b])):
            todo.append(
                pltpu.make_async_copy(
                    source, down.at[b, :, pl.ds(k * half, half)], sems.at[2 * b + k]
                )
            )
    for c in todo:
        c.start()
    for c in todo:
        c.wait()
    tokens = middle.shape[0]
    tile = 128

    def body(i, loss):
        at = span(i * tile, tile)
        there = span(row[0] * tokens + i * tile, tile)
        result = middle[at, :] + bias[...]
        for b in range(4):
            result = result + dot(act[b, at, :], down[b])
        out_own[at, :] = result[:, :half].astype(bf16)
        out_mate[at, :] = result[:, half:].astype(bf16)
        teach = jnp.concatenate([teach_own[there, :], teach_mate[there, :]], axis=1).astype(f32)
        diff = (result - teach) * valid[at, :]
        grad = diff * scale[0]
        grad_ref[at, :] = grad
        low = grad.astype(bf16)
        low_own[at, :] = low[:, :half]
        low_mate[at, :] = low[:, half:]
        for b in range(4):
            upper_ref[b, at, :] = (dot_nt(low, down[b]) * slope[b, at, :].astype(f32)).astype(bf16)
        return loss + jnp.sum(diff * diff, axis=0, keepdims=True)

    loss_ref[...] = lax.fori_loop(
        0, tokens // tile, body, jnp.zeros((1, middle.shape[1]), f32)
    )


def drop(row, scale, act, slope, middle, bias, teach_own, teach_mate, valid, own, mates):
    tokens, width = middle.shape
    half = width // 2
    return call(
        drop_kernel,
        "drop",
        [
            ((tokens, half), bf16),
            ((tokens, half), bf16),
            ((tokens, width), f32),
            ((tokens, half), bf16),
            ((tokens, half), bf16),
            (act.shape, bf16),
            ((1, width), f32),
        ],
        scratch=[pltpu.VMEM((4, width, width), bf16), pltpu.SemaphoreType.DMA((8,))],
        smem=(0, 1),
        hbm=tuple(range(9, 17)),
    )(row, scale, act, slope, middle, bias, teach_own, teach_mate, valid, *own, *mates)


def back_kernel(*refs):
    row, upper, grad_result, middle_ref, gain = refs[:5]
    packs, mates = refs[5:9], refs[9:13]
    grad_own, grad_mate, keep_a, keep_b, give, parts_ref = refs[13:19]
    up, out, sems = refs[19:]
    todo = copies_of_packs(packs, mates, up, out, None, sems)
    for c in todo:
        c.start()
    for c in todo:
        c.wait()
    tokens, width = middle_ref.shape
    half = width // 2
    tile = 128

    def body(i, sums):
        at = span(i * tile, tile)
        grad = dot_nt(upper[0, at, :], up[0])
        for b in range(1, 4):
            grad = grad + dot_nt(upper[b, at, :], up[b])
        middle = middle_ref[at, :]
        center, inverse = norm_stats(middle)
        normed = (middle - center) * inverse
        scaled = grad * gain[...]
        back = grad_result[at, :] + inverse * (
            scaled
            - jnp.mean(scaled, axis=1, keepdims=True)
            - normed * jnp.mean(scaled * normed, axis=1, keepdims=True)
        )
        grad_own[at, :] = back[:, :half]
        grad_mate[at, :] = back[:, half:]
        heads = dot_nt(back.astype(bf16), out[...])
        flip = row[0] == 1
        near, far = heads[:, :half], heads[:, half:]
        keep = jnp.where(flip, far, near).astype(bf16)
        keep_a[at, :] = keep[:, :HEAD_WIDTH]
        keep_b[at, :] = keep[:, HEAD_WIDTH:]
        give[at, :] = jnp.where(flip, near, far).astype(bf16)
        return (
            sums[0] + jnp.sum(grad * normed, axis=0, keepdims=True),
            sums[1] + jnp.sum(grad, axis=0, keepdims=True),
        )

    zero = jnp.zeros((1, width), f32)
    sums = lax.fori_loop(0, tokens // tile, body, (zero, zero))
    parts_ref[0:1, :] = sums[0]
    parts_ref[1:2, :] = sums[1]


def back(row, upper, grad_result, middle, gain, packs, mates):
    tokens, width = middle.shape
    half = width // 2
    return call(
        back_kernel,
        "back",
        [
            ((tokens, half), f32),
            ((tokens, half), f32),
            ((tokens, HEAD_WIDTH), bf16),
            ((tokens, HEAD_WIDTH), bf16),
            ((tokens, half), bf16),
            ((2, width), f32),
        ],
        scratch=[
            pltpu.VMEM((4, width, width), bf16),
            pltpu.VMEM((width, width), bf16),
            pltpu.SemaphoreType.DMA((24,)),
        ],
        smem=(0,),
        hbm=tuple(range(5, 13)),
    )(row, upper, grad_result, middle, gain, *packs, *mates)


def weight_down_kernel(act_own, act_mate, low_own, low_mate, out_ref):
    for b in range(4):
        out_ref[b] = dot_tn(low_own[...], act_own[b]) + dot_tn(low_mate[...], act_mate[b])


def weight_down(act_own, act_mate, low_own, low_mate):
    return call(
        weight_down_kernel, "weight_down", [((4, low_own.shape[1], act_own.shape[2]), f32)]
    )(act_own, act_mate, low_own, low_mate)[0]


def weight_up_kernel(
    row,
    hidden_own,
    hidden_mate,
    upper_own,
    upper_mate,
    chip,
    middle_own,
    middle_mate,
    low_own,
    low_mate,
    parts,
    out_ref,
):
    tokens, half = middle_own.shape
    own = middle_own[...].astype(bf16)
    mate = middle_mate[...].astype(bf16)
    first = chip[span(row[0] * tokens, tokens), :]
    second = chip[span((1 - row[0]) * tokens, tokens), :]
    grad_out = dot_tn(first, own) + dot_tn(second, mate)

    def total(a):
        return jnp.sum(a.astype(f32), axis=0, keepdims=True)

    small = jnp.concatenate(
        [
            jnp.concatenate([parts[0:1, :], parts[1:2, :]], axis=1),
            jnp.concatenate([total(own) + total(mate), total(low_own[...]) + total(low_mate[...])], axis=1),
            jnp.concatenate([parts[2:3, :], parts[3:4, :]], axis=1),
        ],
        axis=0,
    )
    for b in range(4):
        out_ref[b, :UP_ROWS, :] = dot_tn(hidden_own[...], upper_own[b]) + dot_tn(
            hidden_mate[...], upper_mate[b]
        )
        base = b * 2 * OUT_ROWS
        out_ref[b, UP_ROWS : UP_ROWS + OUT_ROWS, :half] = grad_out[base : base + OUT_ROWS]
        out_ref[b, UP_ROWS : UP_ROWS + OUT_ROWS, half:] = grad_out[
            base + OUT_ROWS : base + 2 * OUT_ROWS
        ]
        tail = UP_ROWS + OUT_ROWS
        out_ref[b, tail : tail + 16, :] = jnp.concatenate(
            [total(upper_own[b]) + total(upper_mate[b]), small, jnp.zeros((12, 2 * half), f32)],
            axis=0,
        )


def weight_up(*args):
    width = args[1].shape[1]
    return call(
        weight_up_kernel, "weight_up", [((4, PACK_ROWS, 2 * width), f32)], smem=(0,)
    )(*args)[0]


def unproject_kernel(grads, weights, left, right, gain, keep_ref, give_ref, parts_ref, sums_ref):
    rows = 256
    half = keep_ref.shape[1]

    def step(i, sums):
        at = span(i * rows, rows)
        grad = dot_nt(grads[at, :], weights[...])
        values = jnp.concatenate([left[at, :], right[at, :]], axis=1).astype(f32)
        center, inverse = norm_stats(values)
        normed = (values - center) * inverse
        keep_ref[at, :] = grad[:, :half]
        give_ref[at, :] = grad[:, half:].astype(bf16)
        scaled = grad * gain[...]
        sums_ref[at, 0:1] = jnp.sum(scaled, axis=1, keepdims=True)
        sums_ref[at, 1:2] = jnp.sum(scaled * normed, axis=1, keepdims=True)
        return (
            sums[0] + jnp.sum(grad * normed, axis=0, keepdims=True),
            sums[1] + jnp.sum(grad, axis=0, keepdims=True),
        )

    zero = jnp.zeros((1, 2 * half), f32)
    sums = lax.fori_loop(0, grads.shape[0] // rows, step, (zero, zero))
    parts_ref[0:1, :] = sums[0]
    parts_ref[1:2, :] = sums[1]


def unproject(grads, weights, left, right, gain):
    rows, half = left.shape
    return call(
        unproject_kernel,
        "unproject",
        [((rows, half), f32), ((rows, half), bf16), ((2, 2 * half), f32), ((rows, 2), f32)],
    )(grads, weights, left, right, gain)


def both_halves(own, axis=0):
    return jnp.concatenate([own, send_row(own)], axis=axis)


def on_device(
    states,
    teacher,
    valid_mask,
    seg_ids,
    piece_start,
    norm1_gain,
    norm1_bias,
    w_qkv,
    b_qv,
    w_out,
    b_out,
    norm2_gain,
    norm2_bias,
    w_up,
    b_up,
    w_down,
    b_down,
):
    row = lax.axis_index("row")
    col = lax.axis_index("col")
    half = col % 2
    first = row == 0
    chip_tokens, half_width = states.shape
    tokens = chip_tokens // lax.axis_size("row")
    width = half_width * lax.axis_size("row")
    length = seg_ids.shape[1]
    all_tokens = valid_mask.shape[0] * lax.axis_size("dp")
    blocks = length // BLOCK
    row_word = row[None].astype(jnp.int32)

    states_x = send_x(states)
    states_mate = send_row(states)
    states_x_mate = send_row(states_x)

    bias_high = b_qv.astype(bf16)
    bias_low = (b_qv - bias_high.astype(f32)).astype(bf16)
    zero = jnp.zeros((HEAD_WIDTH,), bf16)
    lines = [jnp.concatenate([b[0], zero, b[1]]) for b in (bias_high, bias_low)]
    qkv_pack = jnp.concatenate(
        [
            w_qkv.reshape(half_width, 3 * HEAD_WIDTH),
            jnp.pad(jnp.stack(lines), ((0, 14), (0, 0))),
        ],
        axis=0,
    )
    qkv_y = send_y(qkv_pack)
    qkv_own = jnp.where(first, qkv_pack, qkv_y)
    qkv_mate = send_row(jnp.where(first, qkv_y, qkv_pack))

    def pad_heads(a):
        a = jnp.pad(a.reshape(a.shape[0], 3, HEAD_WIDTH), ((0, 0), (0, 0), (0, PAD - HEAD_WIDTH)))
        return a.reshape(a.shape[0], 3 * PAD)

    qkv_matrix = pad_heads(jnp.concatenate([qkv_own[:half_width], qkv_mate[:half_width]], axis=0))
    bias_rows = pad_heads(qkv_own[half_width : half_width + 2]).astype(f32)
    qkv_bias = bias_rows[0:1] + bias_rows[1:2]

    def gather_blocks(own):
        over_y = send_y(own)
        over_x = send_x(own)
        return [own, over_x, over_y, send_y(over_x)]

    packs = gather_blocks(pack_up(w_up, w_out, b_up))
    pack_mates = [send_row(p) for p in packs]
    downs = gather_blocks(w_down)
    down_mates = [send_row(p) for p in downs]

    tables = jnp.concatenate([seg_ids, piece_start], axis=0)
    tables = jnp.where(row == col // 2, tables, send_row(tables))
    segs, starts = tables[0], tables[1]
    mask_row = lax.dynamic_slice_in_dim(valid_mask, (col // 2) * length, length)
    places = jnp.arange(length, dtype=jnp.int32)
    ends = [jnp.sum((segs <= s).astype(jnp.int32)) for s in range(3)]
    low = jnp.where(
        segs == 0, 0, jnp.where(segs == 1, ends[0], jnp.where(segs == 2, ends[1], ends[2]))
    )
    high = jnp.where(
        segs == 0, ends[0], jnp.where(segs == 1, ends[1], jnp.where(segs == 2, ends[2], length))
    )
    high = jnp.minimum(high - 1, jnp.maximum(places, starts + PIECE - 1))
    key_ids = jnp.where(mask_row > 0, places, -1)[:, None]
    low_rows = low.reshape(blocks, BLOCK)
    high_rows = high.reshape(blocks, BLOCK)
    half_word = half[None].astype(jnp.int32)
    first_blocks = low_rows[:, 0] // BLOCK
    meta_other = jnp.concatenate([half_word, 1 - half_word, first_blocks])
    meta_own = jnp.concatenate([half_word, half_word, first_blocks])
    meta_back_other = jnp.concatenate([half_word, 1 - half_word, row_word, first_blocks])
    meta_back_own = jnp.concatenate([half_word, half_word, row_word, first_blocks])

    small = both_halves(
        jnp.stack([norm1_gain, norm1_bias, norm2_gain, norm2_bias, b_out, b_down]), axis=1
    )
    gain1, shift1, gain2, shift2, bias_out, bias_down = (small[i : i + 1] for i in range(6))
    count = sum_dp_small(jnp.broadcast_to(jnp.sum(valid_mask.astype(f32)), (8, 128)))[0, 0]
    scale = all_tokens / count

    hidden_own, qkv_a = project(states, states_mate, gain1, shift1, qkv_matrix, qkv_bias)
    hidden_x, qkv_b = project(states_x, states_x_mate, gain1, shift1, qkv_matrix, qkv_bias)

    out_other, wide_other, log_other = attend(
        meta_other, qkv_a, qkv_b, key_ids, low_rows, high_rows
    )
    near_b = send_x(out_other)
    near_a, wide_own, log_own = attend(meta_own, qkv_a, qkv_b, key_ids, low_rows, high_rows)
    far_a, far_b = send_row(near_a), send_row(near_b)

    middle, hidden2, act, slope, chip = lift(
        row_word,
        (near_a, near_b, far_a, far_b),
        states,
        states_mate,
        bias_out,
        gain2,
        shift2,
        packs,
        pack_mates,
    )
    act_mate = send_row(act)
    hidden2_own = hidden2[:, :half_width]
    hidden2_mate = send_row(hidden2[:, half_width:])

    teacher_mate = send_row(teacher)
    valid_rows = lax.dynamic_slice_in_dim(
        valid_mask, col * chip_tokens + row * tokens, tokens
    ).astype(f32)[:, None]
    out_own, out_give, grad_result, low_own, low_give, upper, loss_row = drop(
        row_word,
        scale[None],
        act,
        slope,
        middle,
        bias_down,
        teacher,
        teacher_mate,
        valid_rows,
        downs,
        down_mates,
    )
    low_mate = send_row(low_give)
    upper_mate = send_row(upper)

    def to_chip_rows(own_half, came):
        return jnp.where(
            first,
            jnp.concatenate([own_half, came], axis=0),
            jnp.concatenate([came, own_half], axis=0),
        )

    out = to_chip_rows(out_own, send_row(out_give))

    grad_own, grad_give, keep_a, keep_b, give, parts = back(
        row_word, upper, grad_result, middle, gain2, packs, pack_mates
    )
    came = send_row(give)
    grad_mate = send_row(grad_give)
    came_a, came_b = came[:, :HEAD_WIDTH], came[:, HEAD_WIDTH:]
    across = send_x(jnp.concatenate([keep_b, came_b], axis=0))

    small_own = jnp.concatenate([parts, loss_row], axis=0)
    small_sum = small_own[:, :half_width] + send_row(small_own[:, half_width:])
    small_rows = jnp.concatenate([small_sum, send_row(small_sum[2:3])], axis=0)

    part_down = weight_down(act, act_mate, low_own, low_mate)
    part_up = weight_up(
        row_word,
        hidden2_own,
        hidden2_mate,
        upper,
        upper_mate,
        chip,
        grad_own,
        grad_mate,
        low_own,
        low_mate,
        small_rows,
    )

    def reduce_blocks(part, far_first, near_next):
        part = far_first(part)
        return part[0] + near_next(part[1].astype(bf16)).astype(f32)

    def over_y(part):
        return part[:2] + send_y(part[2:].astype(bf16)).astype(f32)

    def over_x(part):
        pairs = jnp.stack([part[0], part[2]])
        return pairs + send_x(jnp.stack([part[1], part[3]]).astype(bf16)).astype(f32)

    grad_w_down = sum_dp(reduce_blocks(part_down, over_y, send_x)).T
    up_sum = sum_dp(reduce_blocks(part_up, over_x, send_y))
    grad_w_up = up_sum[:UP_ROWS]
    out_sum = up_sum[UP_ROWS : UP_ROWS + OUT_ROWS]
    grad_w_out = jnp.concatenate([out_sum[:, :half_width], out_sum[:, half_width:]], axis=0)
    lines = up_sum[UP_ROWS + OUT_ROWS :]
    grad_b_up = lines[0]
    grad_norm2_gain, grad_norm2_bias = lines[1, :half_width], lines[1, half_width:]
    grad_b_out, grad_b_down = lines[2, :half_width], lines[2, half_width:]
    loss = jnp.sum(lines[3]) / (count * width)

    sums = attend_back(
        meta_back_own,
        qkv_a,
        qkv_b,
        keep_a,
        came_a,
        wide_own,
        log_own,
        key_ids,
        low_rows,
        high_rows,
    )
    dqkv_a, dqkv_b = attend_back(
        meta_back_other,
        qkv_a,
        qkv_b,
        across[:tokens],
        across[tokens:],
        wide_other,
        log_other,
        key_ids,
        low_rows,
        high_rows,
        sums=(sums[1], sums[2], sums[0]),
    )
    keep_x, give_x, parts_x, sums_x = unproject(
        dqkv_b, qkv_matrix, states_x, states_x_mate, gain1
    )
    reduced_x = send_x((keep_x + send_row(give_x).astype(f32)).astype(bf16))
    part_qkv = dot_tn(hidden_own, dqkv_a) + dot_tn(hidden_x, dqkv_b)
    keep_own, give_own, parts_own, sums_own = unproject(
        dqkv_a, qkv_matrix, states, states_mate, gain1
    )
    column_sums = jnp.sum(dqkv_a.astype(f32), axis=0) + jnp.sum(dqkv_b.astype(f32), axis=0)

    def cut(a):
        return a.reshape(a.shape[0], 3, PAD)[:, :, :HEAD_WIDTH].reshape(a.shape[0], 3 * HEAD_WIDTH)

    part_qkv = cut(part_qkv)
    line = jnp.pad(cut(column_sums[None]), ((0, 15), (0, 0)))
    own_half = jnp.concatenate([part_qkv[:half_width], line], axis=0)
    other_half = jnp.concatenate([part_qkv[half_width:], line], axis=0)
    came = send_row(other_half.astype(bf16)).astype(f32)
    stays = jnp.where(first, own_half, came)
    goes = jnp.where(first, came, own_half)
    qkv_sum = sum_dp(stays + send_y(goes.astype(bf16)).astype(f32))
    grad_w_qkv = qkv_sum[:half_width].reshape(w_qkv.shape)
    bias_sum = qkv_sum[half_width].reshape(3, HEAD_WIDTH)
    grad_b_qv = jnp.stack([bias_sum[0], bias_sum[2]])

    sums_own = sums_own + send_row(sums_own)
    sums_x = sums_x + send_row(sums_x)
    token_sums = (sums_own + send_x(sums_x)) / width
    reduced = keep_own + send_row(give_own).astype(f32) + reduced_x.astype(f32)
    middle_chip = to_chip_rows(grad_own, grad_mate)
    values = jnp.concatenate([states, states_mate], axis=1).astype(f32)
    center, inverse = norm_stats(values)
    grad_x = middle_chip + inverse * (
        reduced * gain1[:, :half_width]
        - token_sums[:, 0:1]
        - (states.astype(f32) - center) * inverse * token_sums[:, 1:2]
    )

    late = parts_own + parts_x
    late = late[:, :half_width] + send_row(late[:, half_width:])
    late = late + send_x(late)
    late = late + send_y(late)
    late = sum_dp_small(late)

    return (
        out,
        loss,
        grad_x,
        late[0],
        late[1],
        grad_w_qkv,
        grad_b_qv,
        grad_w_out,
        grad_b_out,
        grad_norm2_gain,
        grad_norm2_bias,
        grad_w_up,
        grad_b_up,
        grad_w_down,
        grad_b_down,
    )


def solution(mesh):
    placed = (
        P(("dp", "col"), "row"),
        P(("dp", "col"), "row"),
        P("dp"),
        P(("dp", "row"), None),
        P(("dp", "row"), None),
        P("row"),
        P("row"),
        P("row", None, "col"),
        P(None, "col"),
        P("col", "row"),
        P("row"),
        P("row"),
        P("row"),
        P("row", "col"),
        P("col"),
        P("col", "row"),
        P("row"),
    )
    return jax.shard_map(
        on_device,
        mesh=mesh,
        in_specs=placed,
        out_specs=(
            P(("dp", "col"), "row"),
            P(),
            P(("dp", "col"), "row"),
            P("row"),
            P("row"),
            P("row", None, "col"),
            P(None, "col"),
            P("col", "row"),
            P("row"),
            P("row"),
            P("row"),
            P("row", "col"),
            P("col"),
            P("col", "row"),
            P("row"),
        ),
        check_vma=False,
    )
```
